768 devices in a mesh: outer: 16 (over y_lo, x, core), inner: 48 (over z, y_hi).
Axes of the slice: x: 4, y: 8 (y_hi: 4, y_lo: 2; y = y_hi * 2 + y_lo), z: 12, core: 2. Of those that a mesh axis runs over, the one named last changes fastest.
Arguments:
- vertex: float32 [196608, 1024], P(('outer', 'inner')), may hold values from -1.5 to 1.5
- vertex_state: float32 [196608], P(('outer', 'inner')), may hold values from 0.05 to 0.5
- context: float32 [196608, 1024], P(('outer', 'inner')), may hold values from -1.5 to 1.5
- context_state: float32 [196608], P(('outer', 'inner')), may hold values from 0.05 to 0.5
- edge_source: int32 [768, 1536], P(('outer', 'inner')), may hold values from 0 to 255
- edge_target: int32 [768, 1536], P(('outer', 'inner')), may hold values from 0 to 255
Outputs:
- vertex_out: float32 [196608, 1024], P(('outer', 'inner'))
- vertex_state_out: float32 [196608], P(('outer', 'inner'))
- context_out: float32 [196608, 1024], P(('outer', 'inner'))
- context_state_out: float32 [196608], P(('outer', 'inner'))
The draws below stay inside these ranges and needn't reach their ends.
All inputs are finite; a program needn't handle non-finite values.
Results may differ from the reference program's by a relative error of at most 0.0019.
Values sent between devices are 32-bit elements; how exact they have to be, the bound alone decides.
No kernel may reach another device: no remote copies, remote signals or barrier semaphores. Data moves between devices by JAX's collectives and lax.ppermute only.
A program may use at most 32 MiB of HBM per device.

```python
import math
import jax
import jax.numpy as jnp
from jax import lax

D = 1024
ROWS = 256
BLK = 256
EDGES = 512
ROUNDS = 3
BUCKETS = 768
N_OUTER = 16
N_INNER = 48


def plant(values, rng, least, top_value):
    extent = values.shape
    place = [jax.random.randint(jax.random.fold_in(rng, axis), (), 0, extent[axis]) for axis in range(len(extent))]
    values = values.at[tuple(place)].set(least)
    longest = extent.index(max(extent))
    place[longest] = (place[longest] + 1) % extent[longest]
    return values.at[tuple(place)].set(top_value)


def shard_levels(key, dims, cuts, smallest, largest):
    loudness = 1.0
    for dim, parts in cuts:
        heights = jax.random.uniform(jax.random.fold_in(jax.random.fold_in(key, 6), dim), (parts,), jnp.float32, smallest / len(cuts), largest / len(cuts))
        loudness = loudness * jnp.repeat(jnp.exp(heights), dims[dim] // parts).reshape((-1,) + (1,) * (len(dims) - 1 - dim))
    return loudness


def gaussian(key, dims, spread, bound, pieces=(), kind=jnp.bfloat16):
    array = jax.random.normal(key, dims, jnp.float32) * spread
    if len(pieces) > 0:
        array = shard_levels(key, dims, pieces, -0.22, 0.18) * array
    return jnp.clip(array, min=-bound, max=bound).astype(kind)


def setup_inputs(seed: int = 0) -> dict:
    splits = jax.random.split(jax.random.key(seed), 7)
    return {
        "vertex": gaussian(splits[0], (BUCKETS * ROWS, D), 0.25, 1.5, ((0, 768),), jnp.float32),
        "vertex_state": jnp.clip(jnp.exp(math.log(0.5) - 2.3025851 * jax.random.uniform(splits[1], (BUCKETS * ROWS,), jnp.float32) ** shard_levels(splits[1], (BUCKETS * ROWS,), ((0, 768),), -0.2, 0.2)), 0.05, 0.5),
        "context": gaussian(splits[2], (BUCKETS * BLK, D), 0.25, 1.5, ((0, 768),), jnp.float32),
        "context_state": jnp.clip(jnp.exp(math.log(0.5) - 2.3025851 * jax.random.uniform(splits[3], (BUCKETS * BLK,), jnp.float32) ** shard_levels(splits[3], (BUCKETS * BLK,), ((0, 768),), -0.2, 0.2)), 0.05, 0.5),
        "edge_source": plant(jax.random.randint(splits[4], (BUCKETS, ROUNDS * EDGES), 0, ROWS), jax.random.fold_in(splits[4], 1), 0, ROWS - 1).astype(jnp.int32),
        "edge_target": plant(jax.random.randint(splits[5], (BUCKETS, ROUNDS * EDGES), 0, BLK), jax.random.fold_in(splits[5], 1), 0, BLK - 1).astype(jnp.int32),
    }


def advance(items):
    rows, row_state, block, block_state, source, target = items
    rows_b = rows.astype(jnp.bfloat16)
    block_b = block.astype(jnp.bfloat16)
    scores = jnp.dot(rows_b, block_b.T, preferred_element_type=jnp.float32)
    prob = jax.nn.sigmoid(scores)
    source_hot = (source[:, None] == jnp.arange(ROWS, dtype=jnp.int32)[None, :]).astype(jnp.bfloat16)
    target_hot = (target[:, None] == jnp.arange(BLK, dtype=jnp.int32)[None, :]).astype(jnp.bfloat16)
    counts = jnp.dot(source_hot.T, target_hot, preferred_element_type=jnp.float32)
    grad = (prob / BLK - counts * (1.0 - prob)).astype(jnp.bfloat16)
    block_grad = jnp.dot(grad.T, rows_b, preferred_element_type=jnp.float32)
    rows_grad = jnp.dot(grad, block_b, preferred_element_type=jnp.float32)
    block_state = block_state + lax.optimization_barrier(jnp.mean(block_grad * block_grad, axis=1))
    block = block - 0.1 * block_grad / jnp.sqrt(block_state)[:, None]
    row_state = row_state + lax.optimization_barrier(jnp.mean(rows_grad * rows_grad, axis=1))
    rows = rows - 0.1 * rows_grad / jnp.sqrt(row_state)[:, None]
    return (rows, row_state, block, block_state)

def reference(vertex, vertex_state, context, context_state, edge_source, edge_target):
    buckets = N_OUTER * N_INNER
    rows = vertex.reshape(buckets, ROWS, D)
    row_state = vertex_state.reshape(buckets, ROWS)
    block = context.reshape(N_OUTER, N_INNER, BLK, D)
    block_state = context_state.reshape(N_OUTER, N_INNER, BLK)
    for step in range(ROUNDS):
        if step > 0:
            block = jnp.roll(block, 1, axis=1)
            block_state = jnp.roll(block_state, 1, axis=1)
        source = edge_source[:, step * EDGES:(step + 1) * EDGES]
        target = edge_target[:, step * EDGES:(step + 1) * EDGES]
        rows, row_state, flat_block, flat_state = lax.map(advance, (rows, row_state, block.reshape(buckets, BLK, D), block_state.reshape(buckets, BLK), source, target), batch_size=16)
        block = flat_block.reshape(N_OUTER, N_INNER, BLK, D)
        block_state = flat_state.reshape(N_OUTER, N_INNER, BLK)
    block = jnp.roll(block, 1, axis=0)
    block_state = jnp.roll(block_state, 1, axis=0)
    return (rows.reshape(buckets * ROWS, D), row_state.reshape(buckets * ROWS), block.reshape(buckets * BLK, D), block_state.reshape(buckets * BLK))
```

```python
import functools

import jax
import jax.numpy as jnp
from jax import lax
from jax.experimental import pallas as pl
from jax.experimental.pallas import tpu as pltpu
from jax.sharding import PartitionSpec as P

ROUNDS = 3
BOTH = ("outer", "inner")
CHUNKS = ((0, 144), (144, 112))
PAD = 8
VMEM = pl.BlockSpec(memory_space=pltpu.VMEM)


def places():
    return lax.axis_size("outer"), lax.axis_size("inner")


def step_inner(n_outer, n_inner):
    return [(o * n_inner + i, o * n_inner + (i + 1) % n_inner) for o in range(n_outer) for i in range(n_inner)]


def step_outer(n_outer, n_inner):
    return [(o * n_inner + i, (o + 1) % n_outer * n_inner + i) for o in range(n_outer) for i in range(n_inner)]


def dot(a, b, contract):
    return lax.dot_general(a, b, (contract, ((), ())), preferred_element_type=jnp.float32)


def hot(index, first, size):
    number = lax.broadcasted_iota(jnp.int32, (size, index.shape[1]), 0) + first
    return jnp.where(number == index, 1.0, 0.0).astype(jnp.bfloat16)


def own_rows(first, size, total):
    row = lax.broadcasted_iota(jnp.int32, (size, total), 0) + first
    return row == lax.broadcasted_iota(jnp.int32, (size, total), 1)


def meet_kernel(first, step, edges, fresh, carry, *refs):
    rows_ref, block_ref, state_ref, source_ref, target_ref, *refs = refs
    before_ref = None
    if first > 0:
        before_ref, *refs = refs
    new_ref, grad_ref, states_ref, *refs = refs
    rows_b = rows_ref[...].astype(jnp.bfloat16)
    if fresh:
        refs[0][...] = rows_b
    size, total = block_ref.shape[0], state_ref.shape[1]
    block = block_ref[...]
    prob = jax.nn.sigmoid(dot(block.astype(jnp.bfloat16), rows_b, ((1,), (1,))))
    window = pl.ds(step * edges, edges)
    counts = dot(hot(target_ref[:, window], first, size), hot(source_ref[:, window], 0, rows_b.shape[0]), ((1,), (1,)))
    grad = (prob / total - counts * (1.0 - prob)).astype(jnp.bfloat16)
    grad_ref[...] = grad
    block_grad = dot(grad, rows_b, ((1,), (0,)))
    mine = own_rows(first, size, total)
    state = jnp.sum(jnp.where(mine, state_ref[...], 0.0), axis=1, keepdims=True)
    state = state + jnp.mean(block_grad * block_grad, axis=1, keepdims=True)
    new_ref[pl.ds(0, size), :] = block - block_grad * (0.1 / jnp.sqrt(state))
    states = jnp.sum(jnp.where(mine, state, 0.0), axis=0, keepdims=True)
    if first > 0:
        states = states + before_ref[...]
    states_ref[...] = states
    if carry:
        new_ref[pl.ds(size, PAD), :] = jnp.zeros((PAD, new_ref.shape[1]), jnp.float32)
        new_ref[pl.ds(size, 1), pl.ds(0, total)] = states


def meet(rows, block, offset, state, source, target, before, first, size, step, last):
    fresh = offset is not None and first == 0
    carry = last and before is not None
    count, width = rows.shape
    edges = source.shape[1] // ROUNDS
    if offset is None:
        spec = VMEM
    else:
        spec = pl.BlockSpec((pl.Element(size), pl.Element(width)), lambda g: (offset, 0))
    out = [
        jax.ShapeDtypeStruct((size + PAD if carry else size, width), jnp.float32),
        jax.ShapeDtypeStruct((size, count), jnp.bfloat16),
        jax.ShapeDtypeStruct(state.shape, jnp.float32),
    ]
    if fresh:
        out.append(jax.ShapeDtypeStruct(rows.shape, jnp.bfloat16))
    args = [rows, block, state, source, target] + ([] if before is None else [before])
    whole = pl.BlockSpec(memory_space=pltpu.VMEM)
    return pl.pallas_call(
        functools.partial(meet_kernel, first, step, edges, fresh, carry),
        grid=(1,),
        out_shape=out,
        in_specs=[whole, spec] + [whole] * (len(args) - 2),
        out_specs=[whole] * len(out),
        cost_estimate=pl.CostEstimate(
            flops=4 * size * count * width, transcendentals=size * count, bytes_accessed=8 * size * width
        ),
        compiler_params=pltpu.CompilerParams(vmem_limit_bytes=24 << 20),
    )(*args)


def bucket_kernel(pieces, *refs):
    rows_ref, state_ref, through_ref, *refs = refs
    grads, blocks = refs[:pieces], refs[pieces : 2 * pieces]
    new_ref, new_state_ref, out_ref, *rounded = refs[2 * pieces :]
    rows_grad = 0.0
    for grad_ref, block_ref in zip(grads, blocks, strict=True):
        rows_grad = rows_grad + dot(grad_ref[...], block_ref[...].astype(jnp.bfloat16), ((0,), (0,)))
    total = state_ref.shape[1]
    mine = own_rows(0, total, total)
    state = jnp.sum(jnp.where(mine, state_ref[...], 0.0), axis=1, keepdims=True)
    state = state + jnp.mean(rows_grad * rows_grad, axis=1, keepdims=True)
    new = rows_ref[...] - rows_grad * (0.1 / jnp.sqrt(state))
    new_ref[...] = new
    if rounded:
        rounded[0][...] = new.astype(jnp.bfloat16)
    new_state_ref[...] = jnp.sum(jnp.where(mine, state, 0.0), axis=0, keepdims=True)
    out_ref[...] = through_ref[...]


def update_bucket(rows, state, through, grads, blocks, offsets, last):
    count, width = rows.shape
    out = [
        jax.ShapeDtypeStruct(rows.shape, jnp.float32),
        jax.ShapeDtypeStruct(state.shape, jnp.float32),
        jax.ShapeDtypeStruct(through.shape, jnp.float32),
    ]
    if not last:
        out.append(jax.ShapeDtypeStruct(rows.shape, jnp.bfloat16))
    whole = pl.BlockSpec(memory_space=pltpu.VMEM)
    specs = []
    for (_, size), offset in zip(CHUNKS, offsets, strict=True):
        if offset is None:
            specs.append(whole)
        else:
            specs.append(
                pl.BlockSpec((pl.Element(size), pl.Element(width)), functools.partial(lambda at, g: (at, 0), offset))
            )
    return pl.pallas_call(
        functools.partial(bucket_kernel, len(grads)),
        grid=(1,),
        out_shape=out,
        in_specs=[whole] * (3 + len(grads)) + specs,
        out_specs=[whole] * len(out),
        cost_estimate=pl.CostEstimate(
            flops=2 * count * count * width, transcendentals=count, bytes_accessed=12 * count * width
        ),
        compiler_params=pltpu.CompilerParams(vmem_limit_bytes=24 << 20),
    )(rows, state, through, *grads, *blocks)


def body(vertex, vertex_state, context, context_state, edge_source, edge_target):
    size = places()
    count = context.shape[0]
    rows, row_state = vertex, vertex_state.reshape(1, -1)
    rounded = vertex
    blocks, offsets = [context] * len(CHUNKS), [a for a, _ in CHUNKS]
    state = context_state.reshape(1, -1)
    for step in range(ROUNDS):
        last = step == ROUNDS - 1
        pairs = step_outer(*size) if last else step_inner(*size)
        moved, grads, states = [], [], None
        for k, (first, n) in enumerate(CHUNKS):
            new, grad, states, *more = meet(
                rounded, blocks[k], offsets[k], state, edge_source, edge_target, states, first, n, step, last
            )
            if more:
                rounded = more[0]
            grads.append(grad)
            moved.append(lax.ppermute(new, BOTH, pairs))
        rows, row_state, states, *more = update_bucket(rows, row_state, states, grads, blocks, offsets, last)
        blocks, offsets = moved, [None] * len(CHUNKS)
        if not last:
            rounded = more[0]
            state = lax.ppermute(states, BOTH, pairs)
    n = CHUNKS[-1][1]
    state = blocks[-1][n, :count]
    block = jnp.concatenate(blocks[:-1] + [blocks[-1][:n]])
    return rows, row_state.reshape(-1), block, state


def solution(mesh):
    flat, table = P(("outer", "inner")), P(("outer", "inner"), None)
    return jax.shard_map(
        body,
        mesh=mesh,
        in_specs=(table, flat, table, flat, table, table),
        out_specs=(table, flat, table, flat),
        check_vma=False,
    )
```

```python
import functools

import jax
import jax.numpy as jnp
from jax import lax
from jax.experimental import pallas as pl
from jax.experimental.pallas import tpu as pltpu
from jax.sharding import PartitionSpec as P

ROUNDS = 3
BOTH = ("outer", "inner")
CHUNKS = ((0, 144), (144, 112))
PAD = 8
LIMIT = 40 << 20
HBM = pl.BlockSpec(memory_space=pltpu.HBM)
VMEM = pl.BlockSpec(memory_space=pltpu.VMEM)


def step_inner(n_outer, n_inner):
    return [(o * n_inner + i, o * n_inner + (i + 1) % n_inner) for o in range(n_outer) for i in range(n_inner)]


def step_outer(n_outer, n_inner):
    return [(o * n_inner + i, (o + 1) % n_outer * n_inner + i) for o in range(n_outer) for i in range(n_inner)]


def dot(a, b, contract):
    return lax.dot_general(a, b, (contract, ((), ())), preferred_element_type=jnp.float32)


def hot(index, first, size):
    number = lax.broadcasted_iota(jnp.int32, (size, index.shape[1]), 0) + first
    return jnp.where(number == index, 1.0, 0.0).astype(jnp.bfloat16)


def own_rows(first, size, total):
    row = lax.broadcasted_iota(jnp.int32, (size, total), 0) + first
    return row == lax.broadcasted_iota(jnp.int32, (size, total), 1)


def edge_counts(source_ref, target_ref, step, edges, first, size, count):
    window = pl.ds(step * edges, edges)
    return dot(hot(target_ref[:, window], first, size), hot(source_ref[:, window], 0, count), ((1,), (1,)))


def update_chunk(first, rows_b, block, state_row, counts, new_ref, grad_ref):
    size, total = block.shape[0], state_row.shape[1]
    prob = jax.nn.sigmoid(dot(block.astype(jnp.bfloat16), rows_b, ((1,), (1,))))
    grad = (prob / total - counts * (1.0 - prob)).astype(jnp.bfloat16)
    grad_ref[...] = grad
    block_grad = dot(grad, rows_b, ((1,), (0,)))
    mine = own_rows(first, size, total)
    state = jnp.sum(jnp.where(mine, state_row, 0.0), axis=1, keepdims=True)
    state = state + jnp.mean(block_grad * block_grad, axis=1, keepdims=True)
    new_ref[pl.ds(0, size), :] = block - block_grad * (0.1 / jnp.sqrt(state))
    new_ref[pl.ds(size, PAD), :] = jnp.zeros((PAD, new_ref.shape[1]), jnp.float32)
    new_ref[pl.ds(size, 1), pl.ds(0, total)] = jnp.sum(jnp.where(mine, state, 0.0), axis=0, keepdims=True)


def first_kernel(first, size, rows_hbm, block_hbm, state_hbm, source_hbm, target_hbm, *refs):
    outs, scratch = refs[:-6], refs[-6:]
    new_ref, grad_ref = outs[0], outs[1]
    rows_ref, block_ref, state_ref, source_ref, target_ref, sems = scratch
    pairs = [
        (source_hbm, source_ref),
        (target_hbm, target_ref),
        (state_hbm, state_ref),
        (rows_hbm, rows_ref),
        (block_hbm.at[pl.ds(first, size), :], block_ref),
    ]
    copies = [pltpu.make_async_copy(a, b, sems.at[k]) for k, (a, b) in enumerate(pairs)]
    for copy in copies:
        copy.start()
    for copy in copies[:3]:
        copy.wait()
    edges = source_ref.shape[1] // ROUNDS
    counts = edge_counts(source_ref, target_ref, 0, edges, first, size, rows_ref.shape[0])
    copies[3].wait()
    rows_b = rows_ref[...].astype(jnp.bfloat16)
    if len(outs) > 2:
        outs[2][...] = rows_b
    copies[4].wait()
    update_chunk(first, rows_b, block_ref[...], state_ref[...], counts, new_ref, grad_ref)


def chunk_outs(size, count, width):
    return [
        jax.ShapeDtypeStruct((size + PAD, width), jnp.float32),
        jax.ShapeDtypeStruct((size, count), jnp.bfloat16),
    ]


def chunk_cost(size, count, width):
    return pl.CostEstimate(
        flops=4 * size * count * width, transcendentals=size * count, bytes_accessed=8 * size * width
    )


def meet_first(rows, context, state, source, target, first, size):
    count, width = rows.shape
    out = chunk_outs(size, count, width)
    if rows.dtype == jnp.float32:
        out.append(jax.ShapeDtypeStruct(rows.shape, jnp.bfloat16))
    return pl.pallas_call(
        functools.partial(first_kernel, first, size),
        out_shape=out,
        in_specs=[HBM if rows.dtype == jnp.float32 else pl.BlockSpec(memory_space=pl.ANY)] + [HBM] * 4,
        out_specs=[VMEM] * len(out),
        scratch_shapes=[
            pltpu.VMEM(rows.shape, rows.dtype),
            pltpu.VMEM((size, width), jnp.float32),
            pltpu.VMEM(state.shape, jnp.float32),
            pltpu.VMEM(source.shape, jnp.int32),
            pltpu.VMEM(target.shape, jnp.int32),
            pltpu.SemaphoreType.DMA((5,)),
        ],
        cost_estimate=chunk_cost(size, count, width),
        compiler_params=pltpu.CompilerParams(vmem_limit_bytes=LIMIT),
    )(rows, context, state, source, target)


def meet_kernel(first, step, edges, rows_ref, block_ref, source_ref, target_ref, *refs):
    new_ref, grad_ref = refs[-2:]
    size, total = grad_ref.shape
    counts = edge_counts(source_ref, target_ref, step, edges, first, size, rows_ref.shape[0])
    state_row = block_ref[pl.ds(size, 1), pl.ds(0, total)]
    update_chunk(first, rows_ref[...], block_ref[pl.ds(0, size), :], state_row, counts, new_ref, grad_ref)


def meet(rows_b, block, source, target, after, first, size, step):
    count, width = rows_b.shape
    out = chunk_outs(size, count, width)
    return pl.pallas_call(
        functools.partial(meet_kernel, first, step, source.shape[1] // ROUNDS),
        out_shape=out,
        in_specs=[VMEM] * 4 + [pl.BlockSpec(memory_space=pl.ANY)] * len(after),
        out_specs=[VMEM] * len(out),
        cost_estimate=chunk_cost(size, count, width),
        compiler_params=pltpu.CompilerParams(vmem_limit_bytes=LIMIT),
    )(rows_b, block, source, target, *after)


def bucket_kernel(sizes, rows_ref, state_ref, *refs):
    pieces = len(sizes)
    grads, blocks = refs[:pieces], refs[pieces : 2 * pieces]
    new_ref, new_state_ref, *rounded = refs[2 * pieces :]
    rows_grad = 0.0
    for (first, size), grad_ref, block_ref in zip(sizes, grads, blocks, strict=True):
        block = block_ref[pl.ds(first, size), :].astype(jnp.bfloat16)
        rows_grad = rows_grad + dot(grad_ref[...], block, ((0,), (0,)))
    total = state_ref.shape[1]
    mine = own_rows(0, total, total)
    state = jnp.sum(jnp.where(mine, state_ref[...], 0.0), axis=1, keepdims=True)
    state = state + jnp.mean(rows_grad * rows_grad, axis=1, keepdims=True)
    new = rows_ref[...] - rows_grad * (0.1 / jnp.sqrt(state))
    new_ref[...] = new
    if rounded:
        rounded[0][...] = new.astype(jnp.bfloat16)
    new_state_ref[...] = jnp.sum(jnp.where(mine, state, 0.0), axis=0, keepdims=True)


def update_bucket(rows, state, grads, blocks, fresh, last):
    count, width = rows.shape
    out = [jax.ShapeDtypeStruct(rows.shape, jnp.float32), jax.ShapeDtypeStruct(state.shape, jnp.float32)]
    if not last:
        out.append(jax.ShapeDtypeStruct(rows.shape, jnp.bfloat16))
    sizes = [(first if fresh else 0, size) for first, size in CHUNKS]
    return pl.pallas_call(
        functools.partial(bucket_kernel, sizes),
        out_shape=out,
        in_specs=[VMEM] * (2 + 2 * len(grads)),
        out_specs=[VMEM] * len(out),
        cost_estimate=pl.CostEstimate(
            flops=2 * count * count * width, transcendentals=count, bytes_accessed=12 * count * width
        ),
        compiler_params=pltpu.CompilerParams(vmem_limit_bytes=LIMIT),
    )(rows, state, *grads, *blocks)


def join_kernel(*refs):
    blocks, (out_ref, state_ref) = refs[:-2], refs[-2:]
    total = state_ref.shape[1]
    states = 0.0
    for (first, size), block_ref in zip(CHUNKS, blocks, strict=True):
        out_ref[pl.ds(first, size), :] = block_ref[pl.ds(0, size), :]
        states = states + block_ref[pl.ds(size, 1), pl.ds(0, total)]
    state_ref[...] = states


def join(blocks, count, width):
    return pl.pallas_call(
        join_kernel,
        out_shape=[jax.ShapeDtypeStruct((count, width), jnp.float32), jax.ShapeDtypeStruct((1, count), jnp.float32)],
        in_specs=[VMEM] * len(blocks),
        out_specs=[VMEM] * 2,
        compiler_params=pltpu.CompilerParams(vmem_limit_bytes=LIMIT),
    )(*blocks)


def body(vertex, vertex_state, context, context_state, edge_source, edge_target):
    size = lax.axis_size("outer"), lax.axis_size("inner")
    count, width = context.shape
    pinned = [pltpu.with_memory_space_constraint(x, pltpu.HBM) for x in (vertex, context, context_state.reshape(1, -1), edge_source, edge_target)]
    rows, row_state, rows_b = vertex, vertex_state.reshape(1, -1), pinned[0]
    blocks = [context] * len(CHUNKS)
    state = context_state.reshape(1, -1)
    for step in range(ROUNDS):
        last = step == ROUNDS - 1
        pairs = step_outer(*size) if last else step_inner(*size)
        moved, grads = [], []
        for k, (first, n) in enumerate(CHUNKS):
            if step == 0:
                new, grad, *more = meet_first(rows_b, *pinned[1:], first, n)
                rows_b = more[0] if more else rows_b
            else:
                new, grad = meet(rows_b, blocks[k], edge_source, edge_target, grads[-1:], first, n, step)
            grads.append(grad)
            moved.append(lax.ppermute(new, BOTH, pairs))
        rows, row_state, *more = update_bucket(rows, row_state, grads, blocks, step == 0, last)
        rows_b = more[0] if more else None
        blocks = moved
    block, state = join(blocks, count, width)
    return rows, row_state.reshape(-1), block, state.reshape(-1)


def solution(mesh):
    flat, table = P(("outer", "inner")), P(("outer", "inner"), None)
    return jax.shard_map(
        body,
        mesh=mesh,
        in_specs=(table, flat, table, flat, table, table),
        out_specs=(table, flat, table, flat),
        check_vma=False,
    )
```

```python
import functools

import jax
import jax.numpy as jnp
from jax import lax
from jax.experimental import pallas as pl
from jax.experimental.pallas import tpu as pltpu
from jax.sharding import PartitionSpec as P

ROUNDS = 3
BOTH = ("outer", "inner")
Y_HI, Y_LO = 4, 2
LANES = 128
STATES = 8
CHUNKS = ((0, 56, False, True), (56, 56, True, False), (112, 72, False, False), (184, 72, False, False))
ORDERS = ((1, 0, 2, 3), (0, 2, 3, 1), (2, 3, 1, 0))
RELAYS = {(1, 2): ((0, 1),), (1, 1): ((1, 0),)}
LIMIT = 40 << 20
HBM = pl.BlockSpec(memory_space=pltpu.HBM)
VMEM = pl.BlockSpec(memory_space=pltpu.VMEM)


def step_inner(n_outer, n_inner):
    return [(o * n_inner + i, o * n_inner + (i + 1) % n_inner) for o in range(n_outer) for i in range(n_inner)]


def step_outer(n_outer, n_inner):
    return [(o * n_inner + i, (o + 1) % n_outer * n_inner + i) for o in range(n_outer) for i in range(n_inner)]


def halfway(n_outer, n_inner):
    share = n_outer // Y_LO
    pairs = []
    for o in range(n_outer):
        for i in range(n_inner):
            y = (i % Y_HI * Y_LO + o // share - 3) % (Y_HI * Y_LO)
            pairs.append((o * n_inner + i, (y % Y_LO * share + o % share) * n_inner + i - i % Y_HI + y // Y_LO))
    return pairs


def dot(a, b, contract):
    return lax.dot_general(a, b, (contract, ((), ())), preferred_element_type=jnp.float32)


def hot(index, first, size):
    number = lax.broadcasted_iota(jnp.int32, (size, index.shape[1]), 0) + first
    return jnp.where(number == index, 1.0, 0.0).astype(jnp.bfloat16)


def own_rows(first, size, total):
    row = lax.broadcasted_iota(jnp.int32, (size, total), 0) + first
    return row == lax.broadcasted_iota(jnp.int32, (size, total), 1)


def edge_counts(source_ref, target_ref, step, edges, first, size, count):
    window = pl.ds(step * edges, edges)
    return dot(hot(target_ref[:, window], first, size), hot(source_ref[:, window], 0, count), ((1,), (1,)))


def unpack(ref, size):
    parts = (ref.shape[0] - STATES) // size
    return jnp.concatenate([ref[pl.ds(k * size, size), :] for k in range(parts)], axis=1)


def unpack_states(ref, total):
    at = ref.shape[0] - STATES
    return jnp.concatenate([ref[pl.ds(at + k, 1), :] for k in range(total // LANES)], axis=1)


def update_chunk(first, rows_b, block, state_row, counts, new_ref, grad_ref):
    size, total = block.shape[0], state_row.shape[1]
    prob = jax.nn.sigmoid(dot(block.astype(jnp.bfloat16), rows_b, ((1,), (1,))))
    grad = (prob / total - counts * (1.0 - prob)).astype(jnp.bfloat16)
    grad_ref[...] = grad
    block_grad = dot(grad, rows_b, ((1,), (0,)))
    mine = own_rows(first, size, total)
    state = jnp.sum(jnp.where(mine, state_row, 0.0), axis=1, keepdims=True)
    state = state + jnp.mean(block_grad * block_grad, axis=1, keepdims=True)
    new = block - block_grad * (0.1 / jnp.sqrt(state))
    states = jnp.sum(jnp.where(mine, state, 0.0), axis=0, keepdims=True)
    parts = block.shape[1] // LANES
    for k in range(parts):
        new_ref[pl.ds(k * size, size), :] = new[:, k * LANES : (k + 1) * LANES]
    new_ref[pl.ds(parts * size, STATES), :] = jnp.zeros((STATES, LANES), jnp.float32)
    for k in range(total // LANES):
        new_ref[pl.ds(parts * size + k, 1), :] = states[:, k * LANES : (k + 1) * LANES]


def first_kernel(first, size, rows_hbm, block_hbm, state_hbm, source_hbm, target_hbm, *refs):
    outs, scratch = refs[:-6], refs[-6:]
    new_ref, grad_ref = outs[0], outs[1]
    rows_ref, block_ref, state_ref, source_ref, target_ref, sems = scratch
    pairs = [
        (source_hbm, source_ref),
        (target_hbm, target_ref),
        (state_hbm, state_ref),
        (rows_hbm, rows_ref),
        (block_hbm.at[pl.ds(first, size), :], block_ref),
    ]
    copies = [pltpu.make_async_copy(a, b, sems.at[k]) for k, (a, b) in enumerate(pairs)]
    for copy in copies:
        copy.start()
    for copy in copies[:3]:
        copy.wait()
    edges = source_ref.shape[1] // ROUNDS
    counts = edge_counts(source_ref, target_ref, 0, edges, first, size, rows_ref.shape[0])
    copies[3].wait()
    rows_b = rows_ref[...].astype(jnp.bfloat16)
    if len(outs) > 2:
        outs[2][...] = rows_b
    copies[4].wait()
    update_chunk(first, rows_b, block_ref[...], state_ref[...], counts, new_ref, grad_ref)


def chunk_outs(size, count, width):
    return [
        jax.ShapeDtypeStruct((size * width // LANES + STATES, LANES), jnp.float32),
        jax.ShapeDtypeStruct((size, count), jnp.bfloat16),
    ]


def chunk_cost(size, count, width):
    return pl.CostEstimate(
        flops=4 * size * count * width, transcendentals=size * count, bytes_accessed=8 * size * width
    )


def meet_first(rows, context, state, source, target, first, size):
    count, width = rows.shape
    out = chunk_outs(size, count, width)
    if rows.dtype == jnp.float32:
        out.append(jax.ShapeDtypeStruct(rows.shape, jnp.bfloat16))
    return pl.pallas_call(
        functools.partial(first_kernel, first, size),
        out_shape=out,
        in_specs=[HBM if rows.dtype == jnp.float32 else pl.BlockSpec(memory_space=pl.ANY)] + [HBM] * 4,
        out_specs=[VMEM] * len(out),
        scratch_shapes=[
            pltpu.VMEM(rows.shape, rows.dtype),
            pltpu.VMEM((size, width), jnp.float32),
            pltpu.VMEM(state.shape, jnp.float32),
            pltpu.VMEM(source.shape, jnp.int32),
            pltpu.VMEM(target.shape, jnp.int32),
            pltpu.SemaphoreType.DMA((5,)),
        ],
        cost_estimate=chunk_cost(size, count, width),
        compiler_params=pltpu.CompilerParams(vmem_limit_bytes=LIMIT),
    )(rows, context, state, source, target)


def meet_kernel(first, step, edges, rows_ref, block_ref, source_ref, target_ref, *refs):
    new_ref, grad_ref = refs[-2:]
    size = grad_ref.shape[0]
    counts = edge_counts(source_ref, target_ref, step, edges, first, size, rows_ref.shape[0])
    state_row = unpack_states(block_ref, rows_ref.shape[0])
    update_chunk(first, rows_ref[...], unpack(block_ref, size), state_row, counts, new_ref, grad_ref)


def meet(rows_b, block, source, target, after, first, size, step):
    count, width = rows_b.shape
    out = chunk_outs(size, count, width)
    return pl.pallas_call(
        functools.partial(meet_kernel, first, step, source.shape[1] // ROUNDS),
        out_shape=out,
        in_specs=[VMEM] * 4 + [pl.BlockSpec(memory_space=pl.ANY)] * len(after),
        out_specs=[VMEM] * len(out),
        cost_estimate=chunk_cost(size, count, width),
        compiler_params=pltpu.CompilerParams(vmem_limit_bytes=LIMIT),
    )(rows_b, block, source, target, *after)


def bucket_kernel(fresh, rows_ref, state_ref, *refs):
    pieces = len(CHUNKS)
    grads, blocks = refs[:pieces], refs[pieces : 2 * pieces]
    new_ref, new_state_ref, *rounded = refs[-2:] if refs[-1].dtype == jnp.float32 else refs[-3:]
    rows_grad = 0.0
    for (first, size, *_), grad_ref, block_ref in zip(CHUNKS, grads, blocks, strict=True):
        block = block_ref[pl.ds(first, size), :] if fresh else unpack(block_ref, size)
        rows_grad = rows_grad + dot(grad_ref[...], block.astype(jnp.bfloat16), ((0,), (0,)))
    total = state_ref.shape[1]
    mine = own_rows(0, total, total)
    state = jnp.sum(jnp.where(mine, state_ref[...], 0.0), axis=1, keepdims=True)
    state = state + jnp.mean(rows_grad * rows_grad, axis=1, keepdims=True)
    new = rows_ref[...] - rows_grad * (0.1 / jnp.sqrt(state))
    new_ref[...] = new
    if rounded:
        rounded[0][...] = new.astype(jnp.bfloat16)
    new_state_ref[...] = jnp.sum(jnp.where(mine, state, 0.0), axis=0, keepdims=True)


def update_bucket(rows, state, grads, blocks, after, fresh, last):
    count, width = rows.shape
    out = [jax.ShapeDtypeStruct(rows.shape, jnp.float32), jax.ShapeDtypeStruct(state.shape, jnp.float32)]
    if not last:
        out.append(jax.ShapeDtypeStruct(rows.shape, jnp.bfloat16))
    return pl.pallas_call(
        functools.partial(bucket_kernel, fresh),
        out_shape=out,
        in_specs=[VMEM] * (2 + 2 * len(grads)) + [pl.BlockSpec(memory_space=pl.ANY)] * len(after),
        out_specs=[VMEM] * len(out),
        cost_estimate=pl.CostEstimate(
            flops=2 * count * count * width, transcendentals=count, bytes_accessed=12 * count * width
        ),
        compiler_params=pltpu.CompilerParams(vmem_limit_bytes=LIMIT),
    )(rows, state, *grads, *blocks, *after)


def join_kernel(*refs):
    blocks, (out_ref, state_ref) = refs[:-2], refs[-2:]
    total = state_ref.shape[1]
    states = 0.0
    for (first, size, *_), block_ref in zip(CHUNKS, blocks, strict=True):
        out_ref[pl.ds(first, size), :] = unpack(block_ref, size)
        states = states + unpack_states(block_ref, total)
    state_ref[...] = states


def join(blocks, count, width):
    return pl.pallas_call(
        join_kernel,
        out_shape=[jax.ShapeDtypeStruct((count, width), jnp.float32), jax.ShapeDtypeStruct((1, count), jnp.float32)],
        in_specs=[VMEM] * len(blocks),
        out_specs=[VMEM] * 2,
        compiler_params=pltpu.CompilerParams(vmem_limit_bytes=LIMIT),
    )(*blocks)


def body(vertex, vertex_state, context, context_state, edge_source, edge_target):
    places = lax.axis_size("outer"), lax.axis_size("inner")
    count, width = context.shape
    direct, relays = step_inner(*places), dict(halfway(*places))
    whole = [vertex, context, context_state.reshape(1, -1), edge_source, edge_target]
    whole = [pltpu.with_memory_space_constraint(array, pltpu.HBM) for array in whole]
    rows, row_state, rows_b = vertex, vertex_state.reshape(1, -1), whole[0]
    blocks = [context] * len(CHUNKS)
    legs = {}
    for step in range(ROUNDS):
        last = step == ROUNDS - 1
        moved, grads, previous = {}, {}, []
        for k in ORDERS[step]:
            first, size, *long_way = CHUNKS[k]
            after = previous + [legs[at] for at in RELAYS.get((step, k), ())]
            if step == 0:
                new, grad, *more = meet_first(rows_b, *whole[1:], first, size)
                rows_b = more[0] if more else rows_b
            else:
                new, grad = meet(rows_b, blocks[k], edge_source, edge_target, after, first, size, step)
            previous, grads[k] = [grad], grad
            if last:
                moved[k] = lax.ppermute(new, BOTH, step_outer(*places))
            elif long_way[step]:
                legs[step, k] = lax.ppermute(new, BOTH, list(relays.items()))
                moved[k] = lax.ppermute(legs[step, k], BOTH, [(relays[p], q) for p, q in direct])
            else:
                moved[k] = lax.ppermute(new, BOTH, direct)
        after = [legs[at] for at in RELAYS.get((step, None), ())]
        grads = [grads[k] for k in range(len(CHUNKS))]
        rows, row_state, *more = update_bucket(rows, row_state, grads, blocks, after, step == 0, last)
        rows_b = more[0] if more else None
        blocks = [moved[k] for k in range(len(CHUNKS))]
    block, state = join(blocks, count, width)
    return rows, row_state.reshape(-1), block, state.reshape(-1)


def solution(mesh):
    flat, table = P(("outer", "inner")), P(("outer", "inner"), None)
    return jax.shard_map(
        body,
        mesh=mesh,
        in_specs=(table, flat, table, flat, table, table),
        out_specs=(table, flat, table, flat),
        check_vma=False,
    )
```

```python
import functools

import jax
import jax.numpy as jnp
from jax import lax
from jax.experimental import pallas as pl
from jax.experimental.pallas import tpu as pltpu
from jax.sharding import PartitionSpec as P

ROUNDS = 3
BOTH = ("outer", "inner")
Y_HI, Y_LO = 4, 2
LANES = 128
STATES = 8
CHUNKS = ((0, 56, False, True), (56, 56, True, False), (112, 72, False, False), (184, 72, False, False))
ORDERS = ((0, 1, 2, 3), (0, 2, 3, 1), (2, 3, 0, 1))
RELAYS = {(1, 2): ((0, 1),), (1, 1): ((1, 0),)}
LIMIT = 40 << 20
HBM = pl.BlockSpec(memory_space=pltpu.HBM)
VMEM = pl.BlockSpec(memory_space=pltpu.VMEM)


def step_inner(n_outer, n_inner):
    return [(o * n_inner + i, o * n_inner + (i + 1) % n_inner) for o in range(n_outer) for i in range(n_inner)]


def step_outer(n_outer, n_inner):
    return [(o * n_inner + i, (o + 1) % n_outer * n_inner + i) for o in range(n_outer) for i in range(n_inner)]


def halfway(n_outer, n_inner):
    share = n_outer // Y_LO
    pairs = []
    for o in range(n_outer):
        for i in range(n_inner):
            y = (i % Y_HI * Y_LO + o // share - 3) % (Y_HI * Y_LO)
            pairs.append((o * n_inner + i, (y % Y_LO * share + o % share) * n_inner + i - i % Y_HI + y // Y_LO))
    return pairs


def mirror(n_outer, n_inner):
    n_z = n_inner // Y_HI
    return [
        (o * n_inner + z * Y_HI + y, o * n_inner + (n_z - 1 - z) * Y_HI + y)
        for o in range(n_outer)
        for z in range((n_z + 1) // 2, n_z)
        for y in range(Y_HI)
    ]


def dot(a, b, contract):
    return lax.dot_general(a, b, (contract, ((), ())), preferred_element_type=jnp.float32)


def hot(index, first, size):
    number = lax.broadcasted_iota(jnp.int32, (size, index.shape[1]), 0) + first
    return jnp.where(number == index, 1.0, 0.0).astype(jnp.bfloat16)


def own_rows(first, size, total):
    row = lax.broadcasted_iota(jnp.int32, (size, total), 0) + first
    return row == lax.broadcasted_iota(jnp.int32, (size, total), 1)


def edge_counts(source_ref, target_ref, step, edges, first, size, count):
    window = pl.ds(step * edges, edges)
    return dot(hot(target_ref[:, window], first, size), hot(source_ref[:, window], 0, count), ((1,), (1,)))


def unpack(ref, size):
    parts = (ref.shape[0] - STATES) // size
    return jnp.concatenate([ref[pl.ds(k * size, size), :] for k in range(parts)], axis=1)


def unpack_states(ref, total):
    at = ref.shape[0] - STATES
    return jnp.concatenate([ref[pl.ds(at + k, 1), :] for k in range(total // LANES)], axis=1)


def update_chunk(first, rows_b, block, state_row, counts, new_ref, grad_ref):
    size, total = block.shape[0], state_row.shape[1]
    prob = jax.nn.sigmoid(dot(block.astype(jnp.bfloat16), rows_b, ((1,), (1,))))
    grad = (prob / total - counts * (1.0 - prob)).astype(jnp.bfloat16)
    grad_ref[...] = grad
    block_grad = dot(grad, rows_b, ((1,), (0,)))
    mine = own_rows(first, size, total)
    state = jnp.sum(jnp.where(mine, state_row, 0.0), axis=1, keepdims=True)
    state = state + jnp.mean(block_grad * block_grad, axis=1, keepdims=True)
    new = block - block_grad * (0.1 / jnp.sqrt(state))
    states = jnp.sum(jnp.where(mine, state, 0.0), axis=0, keepdims=True)
    parts = block.shape[1] // LANES
    for k in range(parts):
        new_ref[pl.ds(k * size, size), :] = new[:, k * LANES : (k + 1) * LANES]
    new_ref[pl.ds(parts * size, STATES), :] = jnp.zeros((STATES, LANES), jnp.float32)
    for k in range(total // LANES):
        new_ref[pl.ds(parts * size + k, 1), :] = states[:, k * LANES : (k + 1) * LANES]


def first_kernel(first, size, rows_hbm, block_hbm, state_hbm, source_hbm, target_hbm, *refs):
    new_ref, grad_ref, rounded_ref, block_ref, state_ref, source_ref, target_ref, rows_ref, sems = refs
    mine = pl.ds(first, size)
    pairs = [
        (source_hbm, source_ref),
        (target_hbm, target_ref),
        (state_hbm, state_ref),
        (rows_hbm, rows_ref),
        (block_hbm.at[mine, :], block_ref.at[mine, :]),
    ]
    count = rows_ref.shape[0]
    if first > 0:
        pairs.append((block_hbm.at[pl.ds(0, first), :], block_ref.at[pl.ds(0, first), :]))
    if first + size < count:
        rest = pl.ds(first + size, count - first - size)
        pairs.append((block_hbm.at[rest, :], block_ref.at[rest, :]))
    copies = [pltpu.make_async_copy(a, b, sems.at[k]) for k, (a, b) in enumerate(pairs)]
    for copy in copies:
        copy.start()
    for copy in copies[:3]:
        copy.wait()
    counts = edge_counts(source_ref, target_ref, 0, source_ref.shape[1] // ROUNDS, first, size, count)
    copies[3].wait()
    rows_b = rows_ref[...].astype(jnp.bfloat16)
    rounded_ref[...] = rows_b
    copies[4].wait()
    update_chunk(first, rows_b, block_ref[mine, :], state_ref[...], counts, new_ref, grad_ref)
    for copy in copies[5:]:
        copy.wait()


def rest_kernel(chunks, rows_ref, block_ref, state_ref, source_ref, target_ref, *refs):
    outs = refs[-2 * len(chunks) :]
    edges = source_ref.shape[1] // ROUNDS
    for (first, size, *_), new_ref, grad_ref in zip(chunks, outs[::2], outs[1::2], strict=True):
        counts = edge_counts(source_ref, target_ref, 0, edges, first, size, rows_ref.shape[0])
        block = block_ref[pl.ds(first, size), :]
        update_chunk(first, rows_ref[...], block, state_ref[...], counts, new_ref, grad_ref)


def chunk_outs(size, count, width):
    return [
        jax.ShapeDtypeStruct((size * width // LANES + STATES, LANES), jnp.float32),
        jax.ShapeDtypeStruct((size, count), jnp.bfloat16),
    ]


def chunk_cost(size, count, width):
    return pl.CostEstimate(
        flops=4 * size * count * width, transcendentals=size * count, bytes_accessed=8 * size * width
    )


def meet_first(rows, context, state, source, target, first, size):
    count, width = rows.shape
    out = chunk_outs(size, count, width) + [jax.ShapeDtypeStruct(rows.shape, jnp.bfloat16)]
    out += [jax.ShapeDtypeStruct(array.shape, array.dtype) for array in (context, state, source, target)]
    return pl.pallas_call(
        functools.partial(first_kernel, first, size),
        out_shape=out,
        in_specs=[HBM] * 5,
        out_specs=[VMEM] * len(out),
        scratch_shapes=[pltpu.VMEM(rows.shape, rows.dtype), pltpu.SemaphoreType.DMA((7,))],
        cost_estimate=chunk_cost(size, count, width),
        compiler_params=pltpu.CompilerParams(vmem_limit_bytes=LIMIT),
    )(rows, context, state, source, target)


def meet_rest(chunks, rows_b, kept, after):
    count, width = rows_b.shape
    out = [shape for _, size, *_ in chunks for shape in chunk_outs(size, count, width)]
    return pl.pallas_call(
        functools.partial(rest_kernel, chunks),
        out_shape=out,
        in_specs=[VMEM] * 5 + [pl.BlockSpec(memory_space=pl.ANY)] * len(after),
        out_specs=[VMEM] * len(out),
        cost_estimate=chunk_cost(sum(size for _, size, *_ in chunks), count, width),
        compiler_params=pltpu.CompilerParams(vmem_limit_bytes=LIMIT),
    )(rows_b, *kept, *after)


def meet_kernel(first, step, edges, rows_ref, block_ref, source_ref, target_ref, *refs):
    new_ref, grad_ref = refs[-2:]
    size = grad_ref.shape[0]
    counts = edge_counts(source_ref, target_ref, step, edges, first, size, rows_ref.shape[0])
    state_row = unpack_states(block_ref, rows_ref.shape[0])
    update_chunk(first, rows_ref[...], unpack(block_ref, size), state_row, counts, new_ref, grad_ref)


def meet(rows_b, block, source, target, after, first, size, step):
    count, width = rows_b.shape
    out = chunk_outs(size, count, width)
    return pl.pallas_call(
        functools.partial(meet_kernel, first, step, source.shape[1] // ROUNDS),
        out_shape=out,
        in_specs=[VMEM] * 4 + [pl.BlockSpec(memory_space=pl.ANY)] * len(after),
        out_specs=[VMEM] * len(out),
        cost_estimate=chunk_cost(size, count, width),
        compiler_params=pltpu.CompilerParams(vmem_limit_bytes=LIMIT),
    )(rows_b, block, source, target, *after)


def bucket_kernel(fresh, rows_ref, state_ref, *refs):
    pieces = len(CHUNKS)
    grads, blocks = refs[:pieces], refs[pieces : 2 * pieces]
    new_ref, new_state_ref, *rounded = refs[-2:] if refs[-1].dtype == jnp.float32 else refs[-3:]
    rows_grad = 0.0
    for (first, size, *_), grad_ref, block_ref in zip(CHUNKS, grads, blocks, strict=True):
        block = block_ref[pl.ds(first, size), :] if fresh else unpack(block_ref, size)
        rows_grad = rows_grad + dot(grad_ref[...], block.astype(jnp.bfloat16), ((0,), (0,)))
    total = state_ref.shape[1]
    mine = own_rows(0, total, total)
    state = jnp.sum(jnp.where(mine, state_ref[...], 0.0), axis=1, keepdims=True)
    state = state + jnp.mean(rows_grad * rows_grad, axis=1, keepdims=True)
    new = rows_ref[...] - rows_grad * (0.1 / jnp.sqrt(state))
    new_ref[...] = new
    if rounded:
        rounded[0][...] = new.astype(jnp.bfloat16)
    new_state_ref[...] = jnp.sum(jnp.where(mine, state, 0.0), axis=0, keepdims=True)


def update_bucket(rows, state, grads, blocks, after, fresh, last):
    count, width = rows.shape
    out = [jax.ShapeDtypeStruct(rows.shape, jnp.float32), jax.ShapeDtypeStruct(state.shape, jnp.float32)]
    if not last:
        out.append(jax.ShapeDtypeStruct(rows.shape, jnp.bfloat16))
    return pl.pallas_call(
        functools.partial(bucket_kernel, fresh),
        out_shape=out,
        in_specs=[VMEM] * (2 + 2 * len(grads)) + [pl.BlockSpec(memory_space=pl.ANY)] * len(after),
        out_specs=[VMEM] * len(out),
        cost_estimate=pl.CostEstimate(
            flops=2 * count * count * width, transcendentals=count, bytes_accessed=12 * count * width
        ),
        compiler_params=pltpu.CompilerParams(vmem_limit_bytes=LIMIT),
    )(rows, state, *grads, *blocks, *after)


def join_kernel(*refs):
    blocks, (out_ref, state_ref) = refs[:-2], refs[-2:]
    total = state_ref.shape[1]
    states = 0.0
    for (first, size, *_), block_ref in zip(CHUNKS, blocks, strict=True):
        out_ref[pl.ds(first, size), :] = unpack(block_ref, size)
        states = states + unpack_states(block_ref, total)
    state_ref[...] = states


def join(blocks, count, width):
    return pl.pallas_call(
        join_kernel,
        out_shape=[jax.ShapeDtypeStruct((count, width), jnp.float32), jax.ShapeDtypeStruct((1, count), jnp.float32)],
        in_specs=[VMEM] * len(blocks),
        out_specs=[VMEM] * 2,
        compiler_params=pltpu.CompilerParams(vmem_limit_bytes=LIMIT),
    )(*blocks)


def body(vertex, vertex_state, context, context_state, edge_source, edge_target):
    places = lax.axis_size("outer"), lax.axis_size("inner")
    count, width = context.shape
    direct, relays = step_inner(*places), dict(halfway(*places))
    whole = [vertex, context, context_state.reshape(1, -1), edge_source, edge_target]
    whole = [pltpu.with_memory_space_constraint(array, pltpu.HBM) for array in whole]
    rows, row_state = vertex, vertex_state.reshape(1, -1)
    signal = lax.ppermute(vertex_state, BOTH, mirror(*places))
    legs = {}
    for step in range(ROUNDS):
        last = step == ROUNDS - 1
        moved, grads, previous = {}, {}, []
        if step == 0:
            front, *others = ORDERS[0]
            new, grad, rows_b, *kept = meet_first(*whole, *CHUNKS[front][:2])
            new, grad, signal = lax.optimization_barrier((new, grad, signal))
            pairs = meet_rest([CHUNKS[k] for k in others], rows_b, kept, [grad, signal])
            met = {front: (new, grad)} | {k: tuple(pairs[2 * j : 2 * j + 2]) for j, k in enumerate(others)}
            blocks, source, target = [kept[0]] * len(CHUNKS), *kept[2:]
        for k in ORDERS[step]:
            first, size, *long_way = CHUNKS[k]
            after = previous + [legs[at] for at in RELAYS.get((step, k), ())]
            if step == 0:
                new, grad = met[k]
            else:
                new, grad = meet(rows_b, blocks[k], source, target, after, first, size, step)
            previous, grads[k] = [grad], grad
            if last:
                moved[k] = lax.ppermute(new, BOTH, step_outer(*places))
            elif long_way[step]:
                legs[step, k] = lax.ppermute(new, BOTH, list(relays.items()))
                moved[k] = lax.ppermute(legs[step, k], BOTH, [(relays[p], q) for p, q in direct])
            else:
                moved[k] = lax.ppermute(new, BOTH, direct)
        after = [legs[at] for at in RELAYS.get((step, None), ())]
        grads = [grads[k] for k in range(len(CHUNKS))]
        rows, row_state, *more = update_bucket(rows, row_state, grads, blocks, after, step == 0, last)
        rows_b = more[0] if more else None
        blocks = [moved[k] for k in range(len(CHUNKS))]
    block, state = join(blocks, count, width)
    return rows, row_state.reshape(-1), block, state.reshape(-1)


def solution(mesh):
    flat, table = P(("outer", "inner")), P(("outer", "inner"), None)
    return jax.shard_map(
        body,
        mesh=mesh,
        in_specs=(table, flat, table, flat, table, table),
        out_specs=(table, flat, table, flat),
        check_vma=False,
    )
```

```python
import functools

import jax
import jax.numpy as jnp
from jax import lax
from jax.experimental import pallas as pl
from jax.experimental.pallas import tpu as pltpu
from jax.sharding import PartitionSpec as P

ROUNDS = 3
BOTH = ("outer", "inner")
Y_HI, Y_LO = 4, 2
LANES = 128
STATES = 8
CHUNKS = ((0, 64, False, True), (64, 56, True, False), (120, 72, False, False), (192, 64, False, False))
ORDERS = (((0,), (1,), (2,), (3,)), ((0,), (2,), (3,), (1,)), ((2, 3), (0, 1)))
RELAYS = {(1, 2): ((0, 1),), (1, 1): ((1, 0),)}
LIMIT = 40 << 20
HBM = pl.BlockSpec(memory_space=pltpu.HBM)
VMEM = pl.BlockSpec(memory_space=pltpu.VMEM)


def step_inner(n_outer, n_inner):
    return [(o * n_inner + i, o * n_inner + (i + 1) % n_inner) for o in range(n_outer) for i in range(n_inner)]


def step_outer(n_outer, n_inner):
    return [(o * n_inner + i, (o + 1) % n_outer * n_inner + i) for o in range(n_outer) for i in range(n_inner)]


def halfway(n_outer, n_inner):
    share = n_outer // Y_LO
    pairs = []
    for o in range(n_outer):
        for i in range(n_inner):
            y = (i % Y_HI * Y_LO + o // share - 3) % (Y_HI * Y_LO)
            pairs.append((o * n_inner + i, (y % Y_LO * share + o % share) * n_inner + i - i % Y_HI + y // Y_LO))
    return pairs


def mirror(n_outer, n_inner):
    n_z = n_inner // Y_HI
    return [
        (o * n_inner + z * Y_HI + y, o * n_inner + (n_z - 1 - z) * Y_HI + y)
        for o in range(n_outer)
        for z in range((n_z + 1) // 2, n_z)
        for y in range(Y_HI)
    ]


def dot(a, b, contract):
    return lax.dot_general(a, b, (contract, ((), ())), preferred_element_type=jnp.float32)


def hot(index, first, size):
    number = lax.broadcasted_iota(jnp.int32, (size, index.shape[1]), 0) + first
    return jnp.where(number == index, 1.0, 0.0).astype(jnp.bfloat16)


def own_rows(first, size, total):
    row = lax.broadcasted_iota(jnp.int32, (size, total), 0) + first
    return row == lax.broadcasted_iota(jnp.int32, (size, total), 1)


def edge_counts(source_ref, target_ref, step, edges, first, size, count):
    window = pl.ds(step * edges, edges)
    return dot(hot(target_ref[:, window], first, size), hot(source_ref[:, window], 0, count), ((1,), (1,)))


def unpack(ref, size):
    parts = (ref.shape[0] - STATES) // size
    return jnp.concatenate([ref[pl.ds(k * size, size), :] for k in range(parts)], axis=1)


def unpack_states(ref, total):
    at = ref.shape[0] - STATES
    return jnp.concatenate([ref[pl.ds(at + k, 1), :] for k in range(total // LANES)], axis=1)


def update_chunk(first, rows_b, block, state_row, counts, new_ref, grad_ref):
    size, total = block.shape[0], state_row.shape[1]
    prob = jax.nn.sigmoid(dot(block.astype(jnp.bfloat16), rows_b, ((1,), (1,))))
    grad = (prob / total - counts * (1.0 - prob)).astype(jnp.bfloat16)
    grad_ref[...] = grad
    block_grad = dot(grad, rows_b, ((1,), (0,)))
    mine = own_rows(first, size, total)
    state = jnp.sum(jnp.where(mine, state_row, 0.0), axis=1, keepdims=True)
    state = state + jnp.mean(block_grad * block_grad, axis=1, keepdims=True)
    new = block - block_grad * (0.1 / jnp.sqrt(state))
    states = jnp.sum(jnp.where(mine, state, 0.0), axis=0, keepdims=True)
    parts = block.shape[1] // LANES
    for k in range(parts):
        new_ref[pl.ds(k * size, size), :] = new[:, k * LANES : (k + 1) * LANES]
    new_ref[pl.ds(parts * size, STATES), :] = jnp.zeros((STATES, LANES), jnp.float32)
    for k in range(total // LANES):
        new_ref[pl.ds(parts * size + k, 1), :] = states[:, k * LANES : (k + 1) * LANES]


def first_kernel(first, size, rows_hbm, block_hbm, state_hbm, source_hbm, target_hbm, *refs):
    new_ref, grad_ref, rounded_ref, block_ref, state_ref, source_ref, target_ref, rows_ref, sems = refs
    mine = pl.ds(first, size)
    pairs = [
        (source_hbm, source_ref),
        (target_hbm, target_ref),
        (state_hbm, state_ref),
        (rows_hbm, rows_ref),
        (block_hbm.at[mine, :], block_ref.at[mine, :]),
    ]
    count = rows_ref.shape[0]
    if first > 0:
        pairs.append((block_hbm.at[pl.ds(0, first), :], block_ref.at[pl.ds(0, first), :]))
    if first + size < count:
        rest = pl.ds(first + size, count - first - size)
        pairs.append((block_hbm.at[rest, :], block_ref.at[rest, :]))
    copies = [pltpu.make_async_copy(a, b, sems.at[k]) for k, (a, b) in enumerate(pairs)]
    for copy in copies:
        copy.start()
    for copy in copies[:3]:
        copy.wait()
    counts = edge_counts(source_ref, target_ref, 0, source_ref.shape[1] // ROUNDS, first, size, count)
    copies[3].wait()
    rows_b = rows_ref[...].astype(jnp.bfloat16)
    rounded_ref[...] = rows_b
    copies[4].wait()
    update_chunk(first, rows_b, block_ref[mine, :], state_ref[...], counts, new_ref, grad_ref)
    for copy in copies[5:]:
        copy.wait()


def rest_kernel(chunks, rows_ref, block_ref, state_ref, source_ref, target_ref, *refs):
    outs = refs[-2 * len(chunks) :]
    edges = source_ref.shape[1] // ROUNDS
    for (first, size, *_), new_ref, grad_ref in zip(chunks, outs[::2], outs[1::2], strict=True):
        counts = edge_counts(source_ref, target_ref, 0, edges, first, size, rows_ref.shape[0])
        block = block_ref[pl.ds(first, size), :]
        update_chunk(first, rows_ref[...], block, state_ref[...], counts, new_ref, grad_ref)


def chunk_outs(size, count, width):
    return [
        jax.ShapeDtypeStruct((size * width // LANES + STATES, LANES), jnp.float32),
        jax.ShapeDtypeStruct((size, count), jnp.bfloat16),
    ]


def chunk_cost(size, count, width):
    return pl.CostEstimate(
        flops=4 * size * count * width, transcendentals=size * count, bytes_accessed=8 * size * width
    )


def meet_first(rows, context, state, source, target, first, size):
    count, width = rows.shape
    out = chunk_outs(size, count, width) + [jax.ShapeDtypeStruct(rows.shape, jnp.bfloat16)]
    out += [jax.ShapeDtypeStruct(array.shape, array.dtype) for array in (context, state, source, target)]
    return pl.pallas_call(
        functools.partial(first_kernel, first, size),
        out_shape=out,
        in_specs=[HBM] * 5,
        out_specs=[VMEM] * len(out),
        scratch_shapes=[pltpu.VMEM(rows.shape, rows.dtype), pltpu.SemaphoreType.DMA((7,))],
        cost_estimate=chunk_cost(size, count, width),
        compiler_params=pltpu.CompilerParams(vmem_limit_bytes=LIMIT),
    )(rows, context, state, source, target)


def meet_rest(chunks, rows_b, kept, after):
    count, width = rows_b.shape
    out = [shape for _, size, *_ in chunks for shape in chunk_outs(size, count, width)]
    return pl.pallas_call(
        functools.partial(rest_kernel, chunks),
        out_shape=out,
        in_specs=[VMEM] * 5 + [pl.BlockSpec(memory_space=pl.ANY)] * len(after),
        out_specs=[VMEM] * len(out),
        cost_estimate=chunk_cost(sum(size for _, size, *_ in chunks), count, width),
        compiler_params=pltpu.CompilerParams(vmem_limit_bytes=LIMIT),
    )(rows_b, *kept, *after)


def meet_kernel(group, step, edges, rows_ref, *refs):
    blocks, (source_ref, target_ref), (new_ref, grad_ref) = refs[: len(group)], refs[len(group) :][:2], refs[-2:]
    first, size, count = group[0][0], grad_ref.shape[0], rows_ref.shape[0]
    counts = edge_counts(source_ref, target_ref, step, edges, first, size, count)
    parts = [unpack(ref, n) for ref, (_, n, *_) in zip(blocks, group, strict=True)]
    state_row = sum(unpack_states(ref, count) for ref in blocks)
    block = parts[0] if len(parts) == 1 else jnp.concatenate(parts, axis=0)
    update_chunk(first, rows_ref[...], block, state_row, counts, new_ref, grad_ref)


def meet(group, rows_b, blocks, source, target, after, step):
    count, width = rows_b.shape
    size = sum(n for _, n, *_ in group)
    out = chunk_outs(size, count, width)
    return pl.pallas_call(
        functools.partial(meet_kernel, group, step, source.shape[1] // ROUNDS),
        out_shape=out,
        in_specs=[VMEM] * (3 + len(blocks)) + [pl.BlockSpec(memory_space=pl.ANY)] * len(after),
        out_specs=[VMEM] * len(out),
        cost_estimate=chunk_cost(size, count, width),
        compiler_params=pltpu.CompilerParams(vmem_limit_bytes=LIMIT),
    )(rows_b, *blocks, source, target, *after)


def bucket_kernel(begins, fresh, rows_ref, state_ref, *refs):
    pieces = len(CHUNKS)
    grads, blocks = refs[:pieces], refs[pieces : 2 * pieces]
    new_ref, new_state_ref, *rounded = refs[-2:] if refs[-1].dtype == jnp.float32 else refs[-3:]
    rows_grad = 0.0
    for (first, size, *_), begin, grad_ref, block_ref in zip(CHUNKS, begins, grads, blocks, strict=True):
        block = block_ref[pl.ds(first, size), :] if fresh else unpack(block_ref, size)
        grad = grad_ref[pl.ds(begin, size), :]
        rows_grad = rows_grad + dot(grad, block.astype(jnp.bfloat16), ((0,), (0,)))
    total = state_ref.shape[1]
    mine = own_rows(0, total, total)
    state = jnp.sum(jnp.where(mine, state_ref[...], 0.0), axis=1, keepdims=True)
    state = state + jnp.mean(rows_grad * rows_grad, axis=1, keepdims=True)
    new = rows_ref[...] - rows_grad * (0.1 / jnp.sqrt(state))
    new_ref[...] = new
    if rounded:
        rounded[0][...] = new.astype(jnp.bfloat16)
    new_state_ref[...] = jnp.sum(jnp.where(mine, state, 0.0), axis=0, keepdims=True)


def update_bucket(rows, state, grads, begins, blocks, after, fresh, last):
    count, width = rows.shape
    out = [jax.ShapeDtypeStruct(rows.shape, jnp.float32), jax.ShapeDtypeStruct(state.shape, jnp.float32)]
    if not last:
        out.append(jax.ShapeDtypeStruct(rows.shape, jnp.bfloat16))
    return pl.pallas_call(
        functools.partial(bucket_kernel, begins, fresh),
        out_shape=out,
        in_specs=[VMEM] * (2 + 2 * len(grads)) + [pl.BlockSpec(memory_space=pl.ANY)] * len(after),
        out_specs=[VMEM] * len(out),
        cost_estimate=pl.CostEstimate(
            flops=2 * count * count * width, transcendentals=count, bytes_accessed=12 * count * width
        ),
        compiler_params=pltpu.CompilerParams(vmem_limit_bytes=LIMIT),
    )(rows, state, *grads, *blocks, *after)


def join_kernel(chunks, *refs):
    blocks, (out_ref, state_ref) = refs[:-2], refs[-2:]
    total = state_ref.shape[1]
    states = 0.0
    for (first, size), block_ref in zip(chunks, blocks, strict=True):
        out_ref[pl.ds(first, size), :] = unpack(block_ref, size)
        states = states + unpack_states(block_ref, total)
    state_ref[...] = states


def join(chunks, blocks, count, width):
    return pl.pallas_call(
        functools.partial(join_kernel, chunks),
        out_shape=[jax.ShapeDtypeStruct((count, width), jnp.float32), jax.ShapeDtypeStruct((1, count), jnp.float32)],
        in_specs=[VMEM] * len(blocks),
        out_specs=[VMEM] * 2,
        compiler_params=pltpu.CompilerParams(vmem_limit_bytes=LIMIT),
    )(*blocks)


def body(vertex, vertex_state, context, context_state, edge_source, edge_target):
    places = lax.axis_size("outer"), lax.axis_size("inner")
    count, width = context.shape
    direct, relays = step_inner(*places), dict(halfway(*places))
    whole = [vertex, context, context_state.reshape(1, -1), edge_source, edge_target]
    whole = [pltpu.with_memory_space_constraint(array, pltpu.HBM) for array in whole]
    rows, row_state = vertex, vertex_state.reshape(1, -1)
    signal = lax.ppermute(vertex_state, BOTH, mirror(*places))
    legs = {}
    for step in range(ROUNDS):
        last = step == ROUNDS - 1
        moved, grads, begins, previous = {}, {}, {}, []
        if step == 0:
            (front,), *others = ORDERS[0]
            others = [k for (k,) in others]
            new, grad, rows_b, *kept = meet_first(*whole, *CHUNKS[front][:2])
            new, grad, signal = lax.optimization_barrier((new, grad, signal))
            pairs = meet_rest([CHUNKS[k] for k in others], rows_b, kept, [grad, signal])
            met = {front: (new, grad)} | {k: tuple(pairs[2 * j : 2 * j + 2]) for j, k in enumerate(others)}
            blocks, source, target = [kept[0]] * len(CHUNKS), *kept[2:]
        for group in ORDERS[step]:
            k, chunks = group[0], [CHUNKS[j] for j in group]
            after = previous + [legs[at] for at in RELAYS.get((step, k), ())]
            if step == 0:
                new, grad = met[k]
            else:
                new, grad = meet(chunks, rows_b, [blocks[j] for j in group], source, target, after, step)
            previous = [grad]
            for place, j in enumerate(group):
                grads[j], begins[j] = grad, sum(n for _, n, *_ in chunks[:place])
            if last:
                moved[chunks[0][0], sum(n for _, n, *_ in chunks)] = lax.ppermute(new, BOTH, step_outer(*places))
            elif chunks[0][2 + step]:
                legs[step, k] = lax.ppermute(new, BOTH, list(relays.items()))
                moved[k] = lax.ppermute(legs[step, k], BOTH, [(relays[p], q) for p, q in direct])
            else:
                moved[k] = lax.ppermute(new, BOTH, direct)
        after = [legs[at] for at in RELAYS.get((step, None), ())]
        grads, begins = ([table[k] for k in range(len(CHUNKS))] for table in (grads, begins))
        rows, row_state, *more = update_bucket(rows, row_state, grads, begins, blocks, after, step == 0, last)
        if not last:
            rows_b = more[0]
            blocks = [moved[k] for k in range(len(CHUNKS))]
    block, state = join(list(moved), list(moved.values()), count, width)
    return rows, row_state.reshape(-1), block, state.reshape(-1)


def solution(mesh):
    flat, table = P(("outer", "inner")), P(("outer", "inner"), None)
    return jax.shard_map(
        body,
        mesh=mesh,
        in_specs=(table, flat, table, flat, table, table),
        out_specs=(table, flat, table, flat),
        check_vma=False,
    )
```

```python
import functools

import jax
import jax.numpy as jnp
from jax import lax
from jax.experimental import pallas as pl
from jax.experimental.pallas import tpu as pltpu
from jax.sharding import PartitionSpec as P

ROUNDS = 3
BOTH = ("outer", "inner")
Y_HI, Y_LO = 4, 2
LEAD = 1
LANES = 128
STATES = 8
CHUNKS = ((0, 56, False, True), (56, 56, True, False), (112, 72, False, False), (184, 72, False, False))
ORDERS = ((0, 1, 2, 3), (0, 2, 3, 1), (2, 3, 0, 1))
RELAYS = {(1, 2): ((0, 1),), (1, 1): ((1, 0),)}
LIMIT = 40 << 20
HBM = pl.BlockSpec(memory_space=pltpu.HBM)
VMEM = pl.BlockSpec(memory_space=pltpu.VMEM)


def step_inner(n_outer, n_inner):
    return [(o * n_inner + i, o * n_inner + (i + 1) % n_inner) for o in range(n_outer) for i in range(n_inner)]


def step_outer(n_outer, n_inner):
    return [(o * n_inner + i, (o + 1) % n_outer * n_inner + i) for o in range(n_outer) for i in range(n_inner)]


def halfway(n_outer, n_inner):
    share = n_outer // Y_LO
    pairs = []
    for o in range(n_outer):
        for i in range(n_inner):
            y = (i % Y_HI * Y_LO + o // share - 3) % (Y_HI * Y_LO)
            pairs.append((o * n_inner + i, (y % Y_LO * share + o % share) * n_inner + i - i % Y_HI + y // Y_LO))
    return pairs


def mirror(n_outer, n_inner):
    top = n_inner // Y_HI - 1 - LEAD
    return [
        (o * n_inner + (top - z) * Y_HI + y, o * n_inner + z * Y_HI + y)
        for o in range(n_outer)
        for z in range((top + 1) // 2)
        for y in range(Y_HI)
    ]


def dot(a, b, contract):
    return lax.dot_general(a, b, (contract, ((), ())), preferred_element_type=jnp.float32)


def hot(index, first, size):
    number = lax.broadcasted_iota(jnp.int32, (size, index.shape[1]), 0) + first
    return jnp.where(number == index, 1.0, 0.0).astype(jnp.bfloat16)


def own_rows(first, size, total):
    row = lax.broadcasted_iota(jnp.int32, (size, total), 0) + first
    return row == lax.broadcasted_iota(jnp.int32, (size, total), 1)


def edge_counts(source_ref, target_ref, step, edges, first, size, count):
    window = pl.ds(step * edges, edges)
    return dot(hot(target_ref[:, window], first, size), hot(source_ref[:, window], 0, count), ((1,), (1,)))


def unpack(ref, size):
    parts = (ref.shape[0] - STATES) // size
    return jnp.concatenate([ref[pl.ds(k * size, size), :] for k in range(parts)], axis=1)


def unpack_states(ref, total):
    at = ref.shape[0] - STATES
    return jnp.concatenate([ref[pl.ds(at + k, 1), :] for k in range(total // LANES)], axis=1)


def update_chunk(first, rows_b, block, state_row, counts, new_ref, grad_ref):
    size, total = block.shape[0], state_row.shape[1]
    prob = jax.nn.sigmoid(dot(block.astype(jnp.bfloat16), rows_b, ((1,), (1,))))
    grad = (prob / total - counts * (1.0 - prob)).astype(jnp.bfloat16)
    grad_ref[...] = grad
    block_grad = dot(grad, rows_b, ((1,), (0,)))
    mine = own_rows(first, size, total)
    state = jnp.sum(jnp.where(mine, state_row, 0.0), axis=1, keepdims=True)
    state = state + jnp.mean(block_grad * block_grad, axis=1, keepdims=True)
    new = block - block_grad * (0.1 / jnp.sqrt(state))
    states = jnp.sum(jnp.where(mine, state, 0.0), axis=0, keepdims=True)
    parts = block.shape[1] // LANES
    for k in range(parts):
        new_ref[pl.ds(k * size, size), :] = new[:, k * LANES : (k + 1) * LANES]
    new_ref[pl.ds(parts * size, STATES), :] = jnp.zeros((STATES, LANES), jnp.float32)
    for k in range(total // LANES):
        new_ref[pl.ds(parts * size + k, 1), :] = states[:, k * LANES : (k + 1) * LANES]


def first_kernel(first, size, rows_hbm, block_hbm, state_hbm, source_hbm, target_hbm, *refs):
    new_ref, grad_ref, rounded_ref, block_ref, state_ref, source_ref, target_ref, rows_ref, sems = refs
    mine = pl.ds(first, size)
    pairs = [
        (source_hbm, source_ref),
        (target_hbm, target_ref),
        (state_hbm, state_ref),
        (rows_hbm, rows_ref),
        (block_hbm.at[mine, :], block_ref.at[mine, :]),
    ]
    count = rows_ref.shape[0]
    if first > 0:
        pairs.append((block_hbm.at[pl.ds(0, first), :], block_ref.at[pl.ds(0, first), :]))
    if first + size < count:
        rest = pl.ds(first + size, count - first - size)
        pairs.append((block_hbm.at[rest, :], block_ref.at[rest, :]))
    copies = [pltpu.make_async_copy(a, b, sems.at[k]) for k, (a, b) in enumerate(pairs)]
    for copy in copies:
        copy.start()
    for copy in copies[:3]:
        copy.wait()
    counts = edge_counts(source_ref, target_ref, 0, source_ref.shape[1] // ROUNDS, first, size, count)
    copies[3].wait()
    rows_b = rows_ref[...].astype(jnp.bfloat16)
    rounded_ref[...] = rows_b
    copies[4].wait()
    update_chunk(first, rows_b, block_ref[mine, :], state_ref[...], counts, new_ref, grad_ref)
    for copy in copies[5:]:
        copy.wait()


def rest_kernel(chunks, rows_ref, block_ref, state_ref, source_ref, target_ref, *refs):
    outs = refs[-2 * len(chunks) :]
    edges = source_ref.shape[1] // ROUNDS
    for (first, size, *_), new_ref, grad_ref in zip(chunks, outs[::2], outs[1::2], strict=True):
        counts = edge_counts(source_ref, target_ref, 0, edges, first, size, rows_ref.shape[0])
        block = block_ref[pl.ds(first, size), :]
        update_chunk(first, rows_ref[...], block, state_ref[...], counts, new_ref, grad_ref)


def chunk_outs(size, count, width):
    return [
        jax.ShapeDtypeStruct((size * width // LANES + STATES, LANES), jnp.float32),
        jax.ShapeDtypeStruct((size, count), jnp.bfloat16),
    ]


def chunk_cost(size, count, width):
    return pl.CostEstimate(
        flops=4 * size * count * width, transcendentals=size * count, bytes_accessed=8 * size * width
    )


def meet_first(rows, context, state, source, target, first, size):
    count, width = rows.shape
    out = chunk_outs(size, count, width) + [jax.ShapeDtypeStruct(rows.shape, jnp.bfloat16)]
    out += [jax.ShapeDtypeStruct(array.shape, array.dtype) for array in (context, state, source, target)]
    return pl.pallas_call(
        functools.partial(first_kernel, first, size),
        out_shape=out,
        in_specs=[HBM] * 5,
        out_specs=[VMEM] * len(out),
        scratch_shapes=[pltpu.VMEM(rows.shape, rows.dtype), pltpu.SemaphoreType.DMA((7,))],
        cost_estimate=chunk_cost(size, count, width),
        compiler_params=pltpu.CompilerParams(vmem_limit_bytes=LIMIT),
    )(rows, context, state, source, target)


def meet_rest(chunks, rows_b, kept, after):
    count, width = rows_b.shape
    out = [shape for _, size, *_ in chunks for shape in chunk_outs(size, count, width)]
    return pl.pallas_call(
        functools.partial(rest_kernel, chunks),
        out_shape=out,
        in_specs=[VMEM] * 5 + [pl.BlockSpec(memory_space=pl.ANY)] * len(after),
        out_specs=[VMEM] * len(out),
        cost_estimate=chunk_cost(sum(size for _, size, *_ in chunks), count, width),
        compiler_params=pltpu.CompilerParams(vmem_limit_bytes=LIMIT),
    )(rows_b, *kept, *after)


def meet_kernel(first, step, edges, rows_ref, block_ref, source_ref, target_ref, *refs):
    new_ref, grad_ref = refs[-2:]
    size = grad_ref.shape[0]
    counts = edge_counts(source_ref, target_ref, step, edges, first, size, rows_ref.shape[0])
    state_row = unpack_states(block_ref, rows_ref.shape[0])
    update_chunk(first, rows_ref[...], unpack(block_ref, size), state_row, counts, new_ref, grad_ref)


def meet(rows_b, block, source, target, after, first, size, step):
    count, width = rows_b.shape
    out = chunk_outs(size, count, width)
    return pl.pallas_call(
        functools.partial(meet_kernel, first, step, source.shape[1] // ROUNDS),
        out_shape=out,
        in_specs=[VMEM] * 4 + [pl.BlockSpec(memory_space=pl.ANY)] * len(after),
        out_specs=[VMEM] * len(out),
        cost_estimate=chunk_cost(size, count, width),
        compiler_params=pltpu.CompilerParams(vmem_limit_bytes=LIMIT),
    )(rows_b, block, source, target, *after)


def bucket_kernel(fresh, rows_ref, state_ref, *refs):
    pieces = len(CHUNKS)
    grads, blocks = refs[:pieces], refs[pieces : 2 * pieces]
    new_ref, new_state_ref, *rounded = refs[-2:] if refs[-1].dtype == jnp.float32 else refs[-3:]
    rows_grad = 0.0
    for (first, size, *_), grad_ref, block_ref in zip(CHUNKS, grads, blocks, strict=True):
        block = block_ref[pl.ds(first, size), :] if fresh else unpack(block_ref, size)
        rows_grad = rows_grad + dot(grad_ref[...], block.astype(jnp.bfloat16), ((0,), (0,)))
    total = state_ref.shape[1]
    mine = own_rows(0, total, total)
    state = jnp.sum(jnp.where(mine, state_ref[...], 0.0), axis=1, keepdims=True)
    state = state + jnp.mean(rows_grad * rows_grad, axis=1, keepdims=True)
    new = rows_ref[...] - rows_grad * (0.1 / jnp.sqrt(state))
    new_ref[...] = new
    if rounded:
        rounded[0][...] = new.astype(jnp.bfloat16)
    new_state_ref[...] = jnp.sum(jnp.where(mine, state, 0.0), axis=0, keepdims=True)


def update_bucket(rows, state, grads, blocks, after, fresh, last):
    count, width = rows.shape
    out = [jax.ShapeDtypeStruct(rows.shape, jnp.float32), jax.ShapeDtypeStruct(state.shape, jnp.float32)]
    if not last:
        out.append(jax.ShapeDtypeStruct(rows.shape, jnp.bfloat16))
    return pl.pallas_call(
        functools.partial(bucket_kernel, fresh),
        out_shape=out,
        in_specs=[VMEM] * (2 + 2 * len(grads)) + [pl.BlockSpec(memory_space=pl.ANY)] * len(after),
        out_specs=[VMEM] * len(out),
        cost_estimate=pl.CostEstimate(
            flops=2 * count * count * width, transcendentals=count, bytes_accessed=12 * count * width
        ),
        compiler_params=pltpu.CompilerParams(vmem_limit_bytes=LIMIT),
    )(rows, state, *grads, *blocks, *after)


def join_kernel(*refs):
    blocks, (out_ref, state_ref) = refs[:-2], refs[-2:]
    total = state_ref.shape[1]
    states = 0.0
    for (first, size, *_), block_ref in zip(CHUNKS, blocks, strict=True):
        out_ref[pl.ds(first, size), :] = unpack(block_ref, size)
        states = states + unpack_states(block_ref, total)
    state_ref[...] = states


def join(blocks, count, width):
    return pl.pallas_call(
        join_kernel,
        out_shape=[jax.ShapeDtypeStruct((count, width), jnp.float32), jax.ShapeDtypeStruct((1, count), jnp.float32)],
        in_specs=[VMEM] * len(blocks),
        out_specs=[VMEM] * 2,
        compiler_params=pltpu.CompilerParams(vmem_limit_bytes=LIMIT),
    )(*blocks)


def body(vertex, vertex_state, context, context_state, edge_source, edge_target):
    places = lax.axis_size("outer"), lax.axis_size("inner")
    count, width = context.shape
    direct, relays = step_inner(*places), dict(halfway(*places))
    whole = [vertex, context, context_state.reshape(1, -1), edge_source, edge_target]
    whole = [pltpu.with_memory_space_constraint(array, pltpu.HBM) for array in whole]
    rows, row_state = vertex, vertex_state.reshape(1, -1)
    signal = lax.ppermute(vertex_state, BOTH, mirror(*places))
    legs = {}
    for step in range(ROUNDS):
        last = step == ROUNDS - 1
        moved, grads, previous = {}, {}, []
        if step == 0:
            front, *others = ORDERS[0]
            new, grad, rows_b, *kept = meet_first(*whole, *CHUNKS[front][:2])
            new, grad, signal = lax.optimization_barrier((new, grad, signal))
            pairs = meet_rest([CHUNKS[k] for k in others], rows_b, kept, [grad, signal])
            met = {front: (new, grad)} | {k: tuple(pairs[2 * j : 2 * j + 2]) for j, k in enumerate(others)}
            blocks, source, target = [kept[0]] * len(CHUNKS), *kept[2:]
        for k in ORDERS[step]:
            first, size, *long_way = CHUNKS[k]
            after = previous + [legs[at] for at in RELAYS.get((step, k), ())]
            if step == 0:
                new, grad = met[k]
            else:
                new, grad = meet(rows_b, blocks[k], source, target, after, first, size, step)
            previous, grads[k] = [grad], grad
            if last:
                moved[k] = lax.ppermute(new, BOTH, step_outer(*places))
            elif long_way[step]:
                legs[step, k] = lax.ppermute(new, BOTH, list(relays.items()))
                moved[k] = lax.ppermute(legs[step, k], BOTH, [(relays[p], q) for p, q in direct])
            else:
                moved[k] = lax.ppermute(new, BOTH, direct)
        after = [legs[at] for at in RELAYS.get((step, None), ())]
        grads = [grads[k] for k in range(len(CHUNKS))]
        rows, row_state, *more = update_bucket(rows, row_state, grads, blocks, after, step == 0, last)
        rows_b = more[0] if more else None
        blocks = [moved[k] for k in range(len(CHUNKS))]
    block, state = join(blocks, count, width)
    return rows, row_state.reshape(-1), block, state.reshape(-1)


def solution(mesh):
    flat, table = P(("outer", "inner")), P(("outer", "inner"), None)
    return jax.shard_map(
        body,
        mesh=mesh,
        in_specs=(table, flat, table, flat, table, table),
        out_specs=(table, flat, table, flat),
        check_vma=False,
    )
```
